32 devices in a mesh: dp: 4 (over z), blk: 8 (over y, x, core).
Axes of the slice: x: 2, y: 2, z: 4, core: 2. Of those that a mesh axis runs over, the one named last changes fastest.
Arguments:
- tokens: bfloat16 [4096, 768], P(('dp', 'blk')), may hold values from -6 to 6
- attn_gain: float32 [768], P(('dp', 'blk')), may hold values from 0.5 to 1.5
- q_weight: float32 [768, 768], P(('dp', 'blk')), may hold values from -0.21875 to 0.21875
- k_weight: float32 [768, 768], P(('dp', 'blk')), may hold values from -0.21875 to 0.21875
- v_weight: float32 [768, 768], P(('dp', 'blk')), may hold values from -0.21875 to 0.21875
- o_weight: float32 [768, 768], P(('dp', 'blk')), may hold values from -1.75 to 1.75
- mlp_gain: float32 [768], P(('dp', 'blk')), may hold values from 0.5 to 1.5
- gate_weight: float32 [768, 3072], P(('dp', 'blk')), may hold values from -0.21875 to 0.21875
- up_weight: float32 [768, 3072], P(('dp', 'blk')), may hold values from -0.21875 to 0.21875
- down_weight: float32 [3072, 768], P(('dp', 'blk')), may hold values from -0.109375 to 0.109375
- doc_lengths: int32 [4, 8], P('dp'), may hold values from 0 to 1024, as said below
- keep: int32 [4096], P(('dp', 'blk')), may hold values 0 or 1
- cotangent: bfloat16 [4096, 768], P(('dp', 'blk')), may hold values from -6 to 6
Outputs:
- layer_out: bfloat16 [4096, 768], P(('dp', 'blk'))
- tokens_grad: bfloat16 [4096, 768], P(('dp', 'blk'))
- attn_gain_grad: float32 [768], P(('dp', 'blk'))
- q_grad: float32 [768, 768], P(('dp', 'blk'))
- k_grad: float32 [768, 768], P(('dp', 'blk'))
- v_grad: float32 [768, 768], P(('dp', 'blk'))
- o_grad: float32 [768, 768], P(('dp', 'blk'))
- mlp_gain_grad: float32 [768], P(('dp', 'blk'))
- gate_grad: float32 [768, 3072], P(('dp', 'blk'))
- up_grad: float32 [768, 3072], P(('dp', 'blk'))
- down_grad: float32 [3072, 768], P(('dp', 'blk'))
The draws below stay inside these ranges and needn't reach their ends.
Inputs may be any that keep to these rules, and one draw needn't show every extreme that they name: `doc_lengths`: each row lists its documents' lengths in order, then zeros; every length is 128, 512 or 1024, and a row's lengths sum to 1024. In every draw some row is a single document of 1024 tokens.
All inputs are finite; a program needn't handle non-finite values. No bound on the sum of `keep` on one device may be relied on, other than what follows from the above.
Results may differ from the reference program's by a relative error of at most 0.014.
The reference program's roundings to bfloat16 on the way count: a program that leaves them out, or rounds other values in their place, can miss the bound.
Values may be sent and summed in bfloat16 or wider, within the bound.
A program may use at most 192 MiB of HBM per device.

```python
import math
import jax
import jax.numpy as jnp
import numpy as np
from jax import lax

D = 768
FF = 3072
H = 12
KVH = 12
HD = 64
ROW = 1024
ROWS = 4
TOKENS = 4096


doc_patterns = np.array([[8, 0, 0, 0, 0, 0, 0, 0], [4, 4, 0, 0, 0, 0, 0, 0], [4, 1, 1, 1, 1, 0, 0, 0], [1, 1, 1, 1, 4, 0, 0, 0], [1, 1, 1, 1, 1, 1, 1, 1], [1, 1, 4, 1, 1, 0, 0, 0]], dtype=np.int32)


def draw_doc_lengths(key, part):
    first_key, second_key = jax.random.split(jax.random.fold_in(key, 7))
    picks = jax.random.randint(first_key, (ROWS,), 0, 6)
    whole_row = jax.random.randint(second_key, (), 0, ROWS)
    picks = jnp.where(jnp.arange(ROWS) == whole_row, 0, picks)
    table = jnp.asarray(doc_patterns)
    chosen = table[picks]
    return (chosen * (ROW // 8)).astype(jnp.int32)


def set_ends(values, own_key, least, largest):
    index_at = [jax.random.randint(jax.random.fold_in(own_key, axis), (), 0, length) for axis, length in enumerate(values.shape)]
    main_axis = values.shape.index(max(values.shape))
    neighbour = index_at[:main_axis] + [(index_at[main_axis] + 1) % values.shape[main_axis]] + index_at[main_axis + 1:]
    return values.at[tuple(index_at)].set(least).at[tuple(neighbour)].set(largest)


def with_spikes(values, key, source, target, blocks, factor):
    owner, partner = [(jnp.arange(values.shape[position]) // (values.shape[position] // blocks)).reshape([-1 if axis == position else 1 for axis in range(values.ndim)]) for position in (source, target)]
    chosen = jax.random.permutation(key, blocks)[partner]
    strong = (owner == chosen) | (owner == (partner + blocks // 2) % blocks)
    return jnp.where(strong, factor * values, values)


def steps_of(rng, shape, shards, least, high):
    gain, own = 1.0, jax.random.fold_in(rng, 6)
    for axis_at, blocks in shards:
        steps = jnp.exp(jax.random.uniform(jax.random.fold_in(own, axis_at), (blocks,), jnp.float32, least / len(shards), high / len(shards)))
        gain = gain * jnp.repeat(steps, shape[axis_at] // blocks).reshape([-1 if axis == axis_at else 1 for axis in range(len(shape))])
    return gain


def bell_draw(key, dims, width, limit, shards=(), held_as=jnp.bfloat16):
    entries = jax.random.normal(key, dims, jnp.float32) * width
    if len(shards) > 0:
        entries = steps_of(key, dims, shards, -0.22, 0.18) * entries
    return jnp.clip(entries, min=-limit, max=limit).astype(held_as)


def bell_draw_with(stream_key, extent, width, reach, cuts, heavy, kind=jnp.bfloat16):
    entries = width * jax.random.normal(stream_key, extent, jnp.float32)
    if cuts:
        entries = entries * steps_of(stream_key, extent, cuts, -0.22, 0.18)
    return jnp.clip(with_spikes(entries, jax.random.fold_in(stream_key, 3), *heavy), -reach, reach).astype(kind)


def setup_inputs(seed: int = 0) -> dict:
    seeds = jax.random.split(jax.random.key(seed), 14)
    tokens = bell_draw_with(seeds[0], (TOKENS, D), 1.0, 6.0, ((0, 32),), (0, 1, 32, 2.75))
    attn_gain = jnp.clip(1.0 + 0.1 * jax.random.normal(seeds[1], (D,), jnp.float32), 0.5, 1.5)
    q_weight = bell_draw(seeds[2], (D, H * HD), D ** -0.5, 0.21875, ((0, 32),), jnp.float32)
    k_weight = bell_draw(seeds[3], (D, KVH * HD), D ** -0.5, 0.21875, ((0, 32),), jnp.float32)
    v_weight = bell_draw(seeds[4], (D, KVH * HD), D ** -0.5, 0.21875, ((0, 32),), jnp.float32)
    o_weight = bell_draw(seeds[5], (H * HD, D), (D // 64) ** -0.5, 1.75, ((0, 32),), jnp.float32)
    mlp_gain = jnp.clip(1.0 + 0.1 * jax.random.normal(seeds[6], (D,), jnp.float32), 0.5, 1.5)
    gate_weight = bell_draw(seeds[7], (D, FF), D ** -0.5, 0.21875, ((0, 32),), jnp.float32)
    up_weight = bell_draw(seeds[8], (D, FF), D ** -0.5, 0.21875, ((0, 32),), jnp.float32)
    down_weight = bell_draw(seeds[9], (FF, D), FF ** -0.5, 0.109375, ((0, 32),), jnp.float32)
    doc_lengths = draw_doc_lengths(jax.random.fold_in(seeds[13], 71), 0)
    keep = set_ends((jax.random.randint(seeds[11], (TOKENS,), 0, 4) < 3).astype(jnp.int32), jax.random.fold_in(seeds[11], 1), 0, 1)
    cotangent = bell_draw(seeds[12], (TOKENS, D), 1.0, 6.0, ((0, 32),))
    return dict(tokens=tokens, attn_gain=attn_gain, q_weight=q_weight, k_weight=k_weight, v_weight=v_weight, o_weight=o_weight, mlp_gain=mlp_gain, gate_weight=gate_weight, up_weight=up_weight, down_weight=down_weight, doc_lengths=doc_lengths, keep=keep, cotangent=cotangent)


EPS = 1e-05
THETA = 10000.0
NEG = -1e+30
HIGH = lax.Precision.HIGHEST

@jax.custom_vjp
def low(v):
    return lax.optimization_barrier(v.astype(jnp.bfloat16)).astype(jnp.float32)

@jax.custom_vjp
def low_back(v):
    return v

def low_keep(v):
    return (low(v), None)

def low_pass(kept, grad):
    return (grad,)

def back_keep(v):
    return (v, None)

def back_low(kept, grad):
    return (low(grad),)
low.defvjp(low_keep, low_pass)
low_back.defvjp(back_keep, back_low)

def angles(in_doc):
    half = HD // 2
    freq = jnp.power(THETA, -jnp.arange(half, dtype=jnp.float32) * 2.0 / HD)
    phase = in_doc.astype(jnp.float32)[:, None] * freq[None, :]
    return (jnp.cos(phase)[:, None, :], jnp.sin(phase)[:, None, :])

def turn(values, cosine, sine):
    count = values.shape[0]
    shaped = values.reshape(count, -1, HD)
    half = HD // 2
    first = shaped[:, :, :half]
    second = shaped[:, :, half:]
    turned = jnp.concatenate([first * cosine - second * sine, second * cosine + first * sine], axis=-1)
    return turned.reshape(count, -1)

def doc_begin(doc_lengths):
    ends = jnp.cumsum(doc_lengths, axis=-1).astype(jnp.int32)
    starts = (ends - doc_lengths).astype(jnp.int32)
    places = jnp.arange(ROW, dtype=jnp.int32)
    inside = (places[None, :, None] >= starts[:, None, :]) & (places[None, :, None] < ends[:, None, :])
    return lax.optimization_barrier(jnp.sum(jnp.where(inside, starts[:, None, :], 0), axis=-1)).astype(jnp.int32)

def attend(q_rot, k_rot, values, begin):
    qblock = min(512, ROW)
    group = H // KVH
    scale = 1.0 / math.sqrt(HD)
    places = jnp.arange(ROW, dtype=jnp.int32)

    def one_row(item):
        q_row, k_row, v_row, begin_row = item
        keys = k_row.reshape(ROW, KVH, HD)
        vals = v_row.reshape(ROW, KVH, HD)

        def one_block(block):
            q_blk, pos_blk, begin_blk = block
            queries = q_blk.reshape(qblock, KVH, group, HD)
            raw = jnp.einsum('qkgd,skd->kgqs', queries, keys, precision=HIGH)
            scores = low_back(raw) * scale
            allow = (places[None, :] <= pos_blk[:, None]) & (places[None, :] >= begin_blk[:, None])
            scores = jnp.where(allow, scores, NEG)
            top = lax.optimization_barrier(jnp.max(scores, axis=-1, keepdims=True))
            expo = jnp.exp(scores - top)
            probs = expo / lax.optimization_barrier(jnp.sum(expo, axis=-1, keepdims=True))
            mixed = jnp.einsum('kgqs,skd->qkgd', low(probs), vals, precision=HIGH)
            return mixed.reshape(qblock, H * HD)
        blocks = (q_row.reshape(ROW // qblock, qblock, H * HD), places.reshape(ROW // qblock, qblock), begin_row.reshape(ROW // qblock, qblock))
        return lax.map(jax.checkpoint(one_block), blocks).reshape(ROW, H * HD)
    rows_in = (q_rot.reshape(ROWS, ROW, H * HD), k_rot.reshape(ROWS, ROW, KVH * HD), values.reshape(ROWS, ROW, KVH * HD), begin)
    return lax.map(jax.checkpoint(one_row), rows_in).reshape(TOKENS, H * HD)

def forward(inputs, attn_gain, q_weight, k_weight, v_weight, o_weight, mlp_gain, gate_weight, up_weight, down_weight, begin, keep_f):
    places = jnp.tile(jnp.arange(ROW, dtype=jnp.int32), ROWS)
    in_doc = places - begin.reshape(TOKENS)
    cosine, sine = angles(in_doc)
    scale1 = lax.rsqrt(lax.optimization_barrier(jnp.mean(inputs * inputs, axis=-1, keepdims=True)) + EPS)
    normed1 = low(inputs * scale1 * low(attn_gain)[None, :])
    queries = low_back(jnp.dot(normed1, low(q_weight), precision=HIGH))
    keys = low_back(jnp.dot(normed1, low(k_weight), precision=HIGH))
    values = low(low_back(jnp.dot(normed1, low(v_weight), precision=HIGH)))
    q_rot = low(turn(queries, cosine, sine))
    k_rot = low(turn(keys, cosine, sine))
    mixed = low(low_back(attend(q_rot, k_rot, values, begin)))
    branch = low_back(jnp.dot(mixed, low(o_weight), precision=HIGH))
    hidden_state = inputs + keep_f * branch
    scale2 = lax.rsqrt(lax.optimization_barrier(jnp.mean(hidden_state * hidden_state, axis=-1, keepdims=True)) + EPS)
    normed2 = low(hidden_state * scale2 * low(mlp_gain)[None, :])
    gate = low_back(jnp.dot(normed2, low(gate_weight), precision=HIGH))
    upper = low_back(jnp.dot(normed2, low(up_weight), precision=HIGH))
    hidden = low(gate * jax.nn.sigmoid(gate) * upper)
    result = low_back(jnp.dot(hidden, low(down_weight), precision=HIGH))
    return hidden_state + keep_f * result

def reference(tokens, attn_gain, q_weight, k_weight, v_weight, o_weight, mlp_gain, gate_weight, up_weight, down_weight, doc_lengths, keep, cotangent):
    begin = doc_begin(doc_lengths)
    keep_f = keep.astype(jnp.float32)[:, None]

    def wrapped(inputs, g_one, w_q, w_k, w_v, w_o, g_two, w_g, w_u, w_d):
        return forward(inputs, g_one, w_q, w_k, w_v, w_o, g_two, w_g, w_u, w_d, begin, keep_f)
    primals = (tokens.astype(jnp.float32), attn_gain, q_weight, k_weight, v_weight, o_weight, mlp_gain, gate_weight, up_weight, down_weight)
    output, pullback = jax.vjp(wrapped, *primals)
    gradients = pullback(cotangent.astype(jnp.float32))
    return (output.astype(jnp.bfloat16), gradients[0].astype(jnp.bfloat16), gradients[1], gradients[2], gradients[3], gradients[4], gradients[5], gradients[6], gradients[7], gradients[8], gradients[9])
```

```python
import functools
import math

import jax
import jax.numpy as jnp
import numpy as np
from jax import lax
from jax.experimental import pallas as pl
from jax.experimental.pallas import tpu as pltpu
from jax.sharding import PartitionSpec as P

H = 12
HD = 64
G = 4
HG = H // G
QG = HG * HD
QKV = 3 * QG
QKVP = 640
EPS = 1e-05
THETA = 10000.0
NEG = -1e30
F32 = jnp.float32
BF = jnp.bfloat16
MESH = pl.DeviceIdType.MESH


def dot_nn(a, b):
    return jnp.dot(a, b, preferred_element_type=F32)


def dot_nt(a, b):
    return lax.dot_general(a, b, (((1,), (1,)), ((), ())), preferred_element_type=F32)


class Place:
    def __init__(self, cf):
        self.cf = cf
        self.d = lax.axis_index("dp")
        self.b = lax.axis_index("blk")
        self.g = self.b // cf.S
        self.s = lax.rem(self.b, cf.S)

    def in_plane(self, k):
        return (self.d, jnp.bitwise_xor(self.g, k) * self.cf.S + self.s)

    def along_z(self, k):
        return (jnp.bitwise_xor(self.d, k), self.b)

    def in_group(self, k):
        return (self.d, self.g * self.cf.S + jnp.bitwise_xor(self.s, k))


class Net:
    def __init__(self, send_sem, recv_sem):
        self.send_sem, self.recv_sem, self.copies = send_sem, recv_sem, []

    def send(self, src, dst, device):
        at = len(self.copies)
        copy = pltpu.make_async_remote_copy(
            src_ref=src,
            dst_ref=dst,
            send_sem=self.send_sem.at[at],
            recv_sem=self.recv_sem.at[at],
            device_id=device,
            device_id_type=MESH,
        )
        copy.start()
        self.copies.append(copy)
        return copy

    def finish(self):
        for copy in self.copies:
            copy.wait_send()


def arrive(copies):
    for copy in copies:
        copy.wait_recv()


def greet(cf, me):
    barrier = pltpu.get_barrier_semaphore()
    peers = [me.in_plane(k) for k in range(1, G)]
    peers += [me.along_z(k) for k in range(1, cf.nd)]
    peers += [me.in_group(k) for k in range(1, cf.S)]
    for peer in peers:
        pl.semaphore_signal(barrier, inc=1, device_id=peer, device_id_type=MESH)
    pl.semaphore_wait(barrier, len(peers))


def keep_column(keep_ref):
    n = keep_ref.shape[1]
    rows = lax.broadcasted_iota(jnp.int32, (n, n), 0)
    lanes = lax.broadcasted_iota(jnp.int32, (n, n), 1)
    keep = keep_ref[...].astype(F32)
    return jnp.sum(jnp.where(rows == lanes, keep, 0.0), axis=1, keepdims=True)


def row_to_column(row):
    n = row.shape[1]
    rows = lax.broadcasted_iota(jnp.int32, (n, n), 0)
    lanes = lax.broadcasted_iota(jnp.int32, (n, n), 1)
    return jnp.sum(jnp.where(rows == lanes, row, 0.0), axis=1, keepdims=True)


def column_to_row(column):
    n = column.shape[0]
    rows = lax.broadcasted_iota(jnp.int32, (n, n), 0)
    lanes = lax.broadcasted_iota(jnp.int32, (n, n), 1)
    return jnp.sum(jnp.where(rows == lanes, column, 0.0), axis=0, keepdims=True)


def doc_begin(len_ref, pos):
    begin = jnp.int32(0)
    start = jnp.int32(0)
    for e in range(len_ref.shape[1]):
        begin = jnp.where(start <= pos, start, begin)
        start = start + len_ref[0, e]
    return begin


def rotary(cf, len_ref, tab_m, tab_r, c):
    pos = c * cf.T
    m = (pos - doc_begin(len_ref, pos)) // cf.T
    cm, sm = tab_m[0, pl.ds(m, 1), :], tab_m[1, pl.ds(m, 1), :]
    cr, sr = tab_r[0], tab_r[1]
    cosine = cm * cr - sm * sr
    sine = sm * cr + cm * sr
    lane = lax.broadcasted_iota(jnp.int32, sine.shape, 1)
    return cosine, jnp.where(lane % HD < HD // 2, -sine, sine)


def swap_halves(slab):
    lane = lax.broadcasted_iota(jnp.int32, slab.shape, 1)
    half = HD // 2
    return jnp.where(lane % HD < half, pltpu.roll(slab, 128 - half, 1), pltpu.roll(slab, half, 1))


def turn(heads, cosine, sine):
    padded = jnp.concatenate([heads, jnp.zeros((heads.shape[0], 256 - QG), F32)], axis=1)
    slabs = [padded[:, at : at + 128] for at in (0, 128)]
    return jnp.concatenate([slab * cosine + swap_halves(slab) * sine for slab in slabs], axis=1)


def kernel_a(
    cf, x_ref, cot_ref, keep_ref, len_ref, g1_ref, g2_ref, wq, wk, wv, wo, wg, wu, tab_m, tab_r,
    WQ, W2, WOF, DYG, XG, XN1, QH, KV, LSE, MIX, HS, XN2, G12,
    W1, WO, PK1, PK2, VT, OH, OS, OX, ssem, rsem,
):
    me = Place(cf)
    d, g, s = me.d, me.g, me.s
    T, S, nd, D = cf.T, cf.S, cf.nd, cf.D
    net = Net(ssem, rsem)
    greet(cf, me)

    gains = jnp.concatenate(
        [row_to_column(g1_ref[...]), row_to_column(g2_ref[...]), jnp.zeros((cf.R, QKVP - QKV - 2), F32)],
        axis=1,
    )
    for t in range(G):
        at = t * QG
        PK1[t] = jnp.concatenate(
            [w[:, at : at + QG] for w in (wq, wk, wv)] + [gains], axis=1
        ).astype(BF)
    W1[d, g, s] = PK1[g]
    first = [net.send(PK1.at[jnp.bitwise_xor(g, k)], W1.at[d, g, s], me.in_plane(k)) for k in (1, 2, 3)]
    XG[g] = x_ref[...]
    tokens = [net.send(x_ref, XG.at[g], me.in_plane(k)) for k in (1, 2, 3)]
    for t in range(G):
        PK2[t] = jnp.concatenate(
            [
                w[:, (G * p + t) * cf.FB : (G * p + t + 1) * cf.FB]
                for w in (wg, wu)
                for p in range(nd)
            ],
            axis=1,
        ).astype(BF)
    W2[d, g, s] = PK2[g]
    second = [net.send(PK2.at[jnp.bitwise_xor(g, k)], W2.at[d, g, s], me.in_plane(k)) for k in (1, 2, 3)]

    arrive(first)
    first_z = [net.send(W1.at[d, :, s], W1.at[d, :, s], me.along_z(k)) for k in range(1, nd)]
    WO[d, g, s] = wo[...].astype(BF)
    out_z = [net.send(WO.at[d, g, s], WO.at[d, g, s], me.along_z(k)) for k in range(1, nd)]
    keep = keep_column(keep_ref)
    DYG[g] = (keep * cot_ref[...].astype(F32)).astype(BF)
    grads = [net.send(DYG.at[g], DYG.at[g], me.in_plane(k)) for k in (1, 2, 3)]
    arrive(second)
    second_z = [net.send(W2.at[d, :, s], W2.at[d, :, s], me.along_z(k)) for k in range(1, nd)]
    arrive(first_z)
    first_s = [net.send(W1.at[:, :, s], W1.at[:, :, s], me.in_group(k)) for k in range(1, S)]
    arrive(out_z)
    out_p = [net.send(WO.at[:, g, s], WO.at[:, g, s], me.in_plane(k)) for k in (1, 2, 3)]
    arrive(first_s)
    WQ[...] = W1[...].reshape(D, QKVP)
    arrive(tokens)
    turned = jnp.transpose(WQ[:, QKVP - 128 : QKVP].astype(F32))
    row = QKV - (QKVP - 128)
    G12[...] = turned[row : row + 8, :]
    gain1 = G12[0:1, :]

    def project(j, unused):
        c = j * S + s
        inputs = XG[j].astype(F32)
        scale1 = lax.rsqrt(jnp.mean(inputs * inputs, axis=-1, keepdims=True) + EPS)
        normed = (inputs * scale1 * gain1).astype(BF)
        XN1[j] = normed
        acc = dot_nn(normed, WQ[...])
        cosine, sine = rotary(cf, len_ref, tab_m, tab_r, c)
        q = turn(acc[:, :QG], cosine, sine).astype(BF)
        k = turn(acc[:, QG : 2 * QG], cosine, sine).astype(BF)
        v = acc[:, 2 * QG : QKV].astype(BF)
        here = pl.ds(pl.multiple_of(c * T, T), T)
        mine = pl.ds(pl.multiple_of(j * T, T), T)
        for h in range(HG):
            QH[h, mine, :] = q[:, h * HD : (h + 1) * HD]
            KV[h, here, :] = k[:, h * HD : (h + 1) * HD]
            KV[HG + h, here, :] = v[:, h * HD : (h + 1) * HD]
        return unused

    lax.fori_loop(0, G, project, 0)
    rows = [
        (c, net.send(KV.at[:, pl.ds(pl.multiple_of((j * S + s) * T, T), T), :],
                     KV.at[:, pl.ds(pl.multiple_of((j * S + s) * T, T), T), :], me.in_group(k)))
        for k in range(1, S) for j in range(G) for c in (0,)
    ]
    arrive(out_p)
    out_s = [net.send(WO.at[:, :, s], WO.at[:, :, s], me.in_group(k)) for k in range(1, S)]
    arrive([copy for unused, copy in rows])

    def attend(h, unused):
        VT[...] = jnp.transpose(KV[HG + h])
        for j in range(G):
            c = j * S + s
            length = (j + 1) * S * T
            begin = doc_begin(len_ref, c * T)
            raw = dot_nt(KV[h, :length, :], QH[h, j * T : (j + 1) * T, :]) * cf.scale
            kpos = lax.broadcasted_iota(jnp.int32, raw.shape, 0)
            qpos = lax.broadcasted_iota(jnp.int32, raw.shape, 1) + c * T
            raw = jnp.where((kpos <= qpos) & (kpos >= begin), raw, NEG)
            top = jnp.max(raw, axis=0, keepdims=True)
            expo = jnp.exp(raw - top)
            total = jnp.sum(expo, axis=0, keepdims=True)
            probs = (expo * (1.0 / total)).astype(BF)
            LSE[h, 0:1, j * T : (j + 1) * T] = top + jnp.log(total)
            mixed = dot_nn(VT[:, :length], probs)
            OH[h, j * T : (j + 1) * T, :] = jnp.transpose(mixed).astype(BF)
        return unused

    lax.fori_loop(0, HG, attend, 0)
    for j in range(G):
        OS[j] = jnp.concatenate([OH[h, j * T : (j + 1) * T, :] for h in range(HG)], axis=1)
    OX[g] = OS[g]
    heads = [net.send(OS.at[jnp.bitwise_xor(g, k)], OX.at[g], me.in_plane(k)) for k in (1, 2, 3)]
    arrive(out_s)
    WOF[...] = WO[...].reshape(D, D)
    arrive(heads)
    MIX[...] = jnp.concatenate([OX[t] for t in range(G)], axis=1)
    state = x_ref[...].astype(F32) + keep * dot_nn(MIX[...], WOF[...])
    HS[...] = state
    scale2 = lax.rsqrt(jnp.mean(state * state, axis=-1, keepdims=True) + EPS)
    XN2[...] = (state * scale2 * G12[1:2, :]).astype(BF)
    arrive(second_z)
    second_s = [net.send(W2.at[:, :, s], W2.at[:, :, s], me.in_group(k)) for k in range(1, S)]
    arrive(grads)
    arrive(second_s)
    net.finish()


def kernel_b(
    cf, XN2, DYG, W2, wd, HS, cot_ref, keep_ref, G12, WOF, MIX,
    YS, YO, DH, DO, GU, GD, GO, MG,
    X2G, WD, WDF, HID, DGU, XT, HT, MT, DXF, DXS, RDX, ssem, rsem,
):
    me = Place(cf)
    d, g, s = me.d, me.g, me.s
    T, S, nd, D, FG = cf.T, cf.S, cf.nd, cf.D, cf.FG
    TT = G * T
    net = Net(ssem, rsem)
    greet(cf, me)
    X2G[g] = XN2[...]
    acts = [net.send(XN2, X2G.at[g], me.in_plane(k)) for k in (1, 2, 3)]
    WD[d, s] = wd[...].astype(BF)
    down_z = [net.send(WD.at[d, s], WD.at[d, s], me.along_z(k)) for k in range(1, nd)]
    keep = keep_column(keep_ref)
    arrive(down_z)
    down_s = [net.send(WD.at[:, s], WD.at[:, s], me.in_group(k)) for k in range(1, S)]
    arrive(acts)
    arrive(down_s)
    WDF[...] = WD[...].reshape(FG, D)

    def tile(n):
        return pl.ds(pl.multiple_of(n * 256, 256), 256)

    def middle(n, unused):
        x = X2G[...].reshape(TT, D)
        gate = dot_nn(x, W2[:, tile(n)])
        up = dot_nn(x, W2[:, tile(n + FG // 256)])
        dhid = dot_nt(DYG[...].reshape(TT, D), WDF[tile(n), :])
        sig = jax.nn.sigmoid(gate)
        HID[:, tile(n)] = (gate * sig * up).astype(BF)
        DGU[:, tile(n)] = (dhid * up * sig * (1.0 + gate * (1.0 - sig))).astype(BF)
        DGU[:, tile(n + FG // 256)] = (dhid * gate * sig).astype(BF)
        return unused

    lax.fori_loop(0, FG // 256, middle, 0)

    def back(n, unused):
        part = dot_nt(DGU[...], W2[tile(n), :])
        DXF[:, tile(n)] = part
        DXS[:, :, tile(n)] = part.astype(BF).reshape(G, T, 256)
        return unused

    lax.fori_loop(0, D // 256, back, 0)
    sums = [net.send(DXS.at[jnp.bitwise_xor(g, k)], RDX.at[k - 1], me.in_plane(k)) for k in (1, 2, 3)]

    XT[...] = jnp.transpose(X2G[...].reshape(TT, D))
    HT[...] = jnp.transpose(HID[...])
    MT[...] = jnp.transpose(MIX[...])

    def weight_grads(n, unused):
        GU[:, tile(n)] = dot_nn(XT[...], DGU[:, tile(n)]).astype(BF)
        return unused

    lax.fori_loop(0, 2 * FG // 256, weight_grads, 0)

    def down_grads(n, unused):
        GD[:, tile(n)] = dot_nn(HT[...], DYG[:, :, tile(n)].reshape(TT, 256)).astype(BF)
        y = dot_nn(HID[...], WDF[:, tile(n)])
        YS[:, :, tile(n)] = y.astype(BF).reshape(G, T, 256)
        return unused

    lax.fori_loop(0, D // 256, down_grads, 0)
    mine = pl.ds(pl.multiple_of(g * T, T), T)
    YO[...] = dot_nn(HID[mine, :], WDF[...])

    arrive(sums)
    dxn2 = DXF[mine, :]
    for k in (1, 2, 3):
        dxn2 = dxn2 + RDX[k - 1].astype(F32)
    state = HS[...]
    scale2 = lax.rsqrt(jnp.mean(state * state, axis=-1, keepdims=True) + EPS)
    hhat = state * scale2
    MG[...] = jnp.broadcast_to(jnp.sum(dxn2 * hhat, axis=0, keepdims=True), MG.shape)
    dhh = dxn2 * G12[1:2, :]
    dh = cot_ref[...].astype(F32) + scale2 * (dhh - hhat * jnp.mean(dhh * hhat, axis=-1, keepdims=True))
    DH[...] = dh
    da = (keep * dh).astype(BF)
    DO[...] = dot_nt(da, WOF[...]).astype(BF)
    GO[...] = dot_nn(MT[...], da).astype(BF)
    net.finish()


def kernel_c(
    cf, x_ref, keep_ref, len_ref, tab_m, tab_r, WQ, XG, XN1, QH, KV, LSE, HS, G12, YS, YO, DH, DO, GU, GD, GO, MG,
    layer_out, tokens_grad, ga, gq, gk, gv, go, gm, gg, gu, gd,
    DOS, DOG, DOH, RY, RGU, RGD, RGO, ZGU, ZGD, NGO, ZGO, OGU, OGO, KT, DKV, DQ, DKS, RDK, DQKV, DXF, DXS, RDX,
    XT, GQ, RGQ, ZGQ, OGQ, ssem, rsem,
):
    me = Place(cf)
    d, g, s = me.d, me.g, me.s
    T, S, nd, D, R, FG, FB = cf.T, cf.S, cf.nd, cf.D, cf.R, cf.FG, cf.FB
    TT = G * T
    net = Net(ssem, rsem)
    other = lambda k: jnp.bitwise_xor(g, k)
    plane = lambda k: jnp.bitwise_xor(d, k)
    sub = lambda k: jnp.bitwise_xor(s, k)
    greet(cf, me)
    do = DO[...]
    for t in range(G):
        DOS[t] = do[:, t * QG : (t + 1) * QG]
    DOG[g] = DOS[g]
    heads = [net.send(DOS.at[other(k)], DOG.at[g], me.in_plane(k)) for k in (1, 2, 3)]
    subs = range(1, S)
    pair_u = [net.send(GU.at[:, :, sub(k)], RGU.at[k - 1], me.in_group(k)) for k in subs]
    pair_d = [net.send(GD.at[:, sub(k)], RGD.at[k - 1], me.in_group(k)) for k in subs]
    pair_o = [net.send(GO.at[:, :, sub(k)], RGO.at[k - 1], me.in_group(k)) for k in subs]
    outs = [net.send(YS.at[other(k)], RY.at[k - 1], me.in_plane(k)) for k in (1, 2, 3)]

    arrive(pair_u)

    def add_u(i, unused):
        p, t = i // G, lax.rem(i, G)
        total = GU[p, t, s].astype(F32)
        for k in subs:
            total = total + RGU[k - 1, p, t].astype(F32)
        RGU[0, p, t] = total.astype(BF)
        return unused

    lax.fori_loop(0, nd * G, add_u, 0)
    z_u = [net.send(RGU.at[0, plane(k)], ZGU.at[k - 1], me.along_z(k)) for k in range(1, nd)]
    arrive(pair_d)

    def add_d(p, unused):
        total = GD[p, s].astype(F32)
        for k in subs:
            total = total + RGD[k - 1, p].astype(F32)
        RGD[0, p] = total.astype(BF)
        return unused

    lax.fori_loop(0, nd, add_d, 0)
    z_d = [net.send(RGD.at[0, plane(k)], ZGD.at[k - 1], me.along_z(k)) for k in range(1, nd)]
    arrive(pair_o)

    def add_o(i, unused):
        p, t = i // G, lax.rem(i, G)
        total = GO[p, t, s].astype(F32)
        for k in subs:
            total = total + RGO[k - 1, p, t].astype(F32)
        RGO[0, p, t] = total.astype(BF)
        return unused

    lax.fori_loop(0, nd * G, add_o, 0)
    plane_o = [net.send(RGO.at[0, :, other(k)], NGO.at[k - 1], me.in_plane(k)) for k in (1, 2, 3)]

    arrive(heads)
    for j in range(G):
        for h in range(HG):
            DOH[h, j * T : (j + 1) * T, :] = DOG[j, :, h * HD : (h + 1) * HD]

    def attend(h, unused):
        KT[...] = jnp.transpose(KV[h])
        for j in range(G - 1, -1, -1):
            c = j * S + s
            length = (j + 1) * S * T
            mine = slice(j * T, (j + 1) * T)
            begin = doc_begin(len_ref, c * T)
            q, dout = QH[h, mine, :], DOH[h, mine, :]
            raw = dot_nt(KV[h, :length, :], q) * cf.scale
            kpos = lax.broadcasted_iota(jnp.int32, raw.shape, 0)
            qpos = lax.broadcasted_iota(jnp.int32, raw.shape, 1) + c * T
            allow = (kpos <= qpos) & (kpos >= begin)
            probs = jnp.where(allow, jnp.exp(raw - LSE[h, 0:1, mine]), 0.0)
            dprobs = dot_nt(KV[HG + h, :length, :], dout)
            delta = jnp.sum(probs * dprobs, axis=0, keepdims=True)
            dscores = (probs * (dprobs - delta) * cf.scale).astype(BF)
            dk = dot_nn(dscores, q)
            dv = dot_nn(probs.astype(BF), dout)
            if j < G - 1:
                dk = dk + DKV[h, :length, :]
                dv = dv + DKV[HG + h, :length, :]
            DKV[h, :length, :] = dk
            DKV[HG + h, :length, :] = dv
            DQ[h, mine, :] = jnp.transpose(dot_nn(KT[:, :length], dscores))
        return unused

    lax.fori_loop(0, HG, attend, 0)
    for k in subs:
        for j in range(G):
            rows = pl.ds(pl.multiple_of((j * S + sub(k)) * T, T), T)
            DKS[k - 1, :, j * T : (j + 1) * T, :] = DKV[:, rows, :].astype(BF)
    pair_k = [net.send(DKS.at[k - 1], RDK.at[k - 1], me.in_group(k)) for k in subs]
    XT[...] = jnp.transpose(XN1[...].reshape(TT, D))

    arrive(plane_o)

    def sum_o(p, unused):
        total = RGO[0, p, g].astype(F32)
        for k in (1, 2, 3):
            total = total + NGO[k - 1, p].astype(F32)
        OGO[p] = total.astype(BF)
        return unused

    lax.fori_loop(0, nd, sum_o, 0)
    z_o = [net.send(OGO.at[plane(k)], ZGO.at[k - 1], me.along_z(k)) for k in range(1, nd)]

    arrive(pair_k)
    for j in range(G):
        c = j * S + s
        rows = pl.ds(pl.multiple_of(c * T, T), T)
        mine = slice(j * T, (j + 1) * T)
        cosine, sine = rotary(cf, len_ref, tab_m, tab_r, c)
        whole = []
        for h in range(2 * HG):
            total = DKV[h, rows, :]
            for k in subs:
                total = total + RDK[k - 1, h, mine, :].astype(F32)
            whole.append(total)
        dq = jnp.concatenate([DQ[h, mine, :] for h in range(HG)], axis=1)
        dq = turn(dq, cosine, -sine)[:, :QG]
        dk = turn(jnp.concatenate(whole[:HG], axis=1), cosine, -sine)[:, :QG]
        DQKV[mine, :] = jnp.concatenate(
            [dq, dk] + whole[HG:] + [jnp.zeros((T, QKVP - QKV), F32)], axis=1
        ).astype(BF)

    def tile(n):
        return pl.ds(pl.multiple_of(n * 256, 256), 256)

    def back(n, unused):
        part = dot_nt(DQKV[...], WQ[tile(n), :])
        DXF[:, tile(n)] = part
        DXS[:, :, tile(n)] = part.astype(BF).reshape(G, T, 256)
        return unused

    lax.fori_loop(0, D // 256, back, 0)
    sums = [net.send(DXS.at[other(k)], RDX.at[k - 1], me.in_plane(k)) for k in (1, 2, 3)]

    def gain(j, total):
        inputs = XG[j].astype(F32)
        scale1 = lax.rsqrt(jnp.mean(inputs * inputs, axis=-1, keepdims=True) + EPS)
        part = DXF[pl.ds(pl.multiple_of(j * T, T), T), :]
        return total + jnp.sum(part * (inputs * scale1), axis=0, keepdims=True)

    gain_row = lax.fori_loop(0, G, gain, jnp.zeros((1, D), F32))
    spare = QKV - (QKVP - 128)
    rows = lax.broadcasted_iota(jnp.int32, (128, D), 0)
    gain_rows = jnp.where(rows == spare, gain_row, jnp.where(rows == spare + 1, MG[0:1, :], 0.0))
    products = [dot_nn(XT[...], DQKV[:, at : at + 128]) for at in range(0, QKVP, 128)]
    products[-1] = products[-1] + jnp.transpose(gain_rows)
    GQ[...] = jnp.concatenate([p.astype(BF) for p in products], axis=1).reshape(nd, G, S, R, QKVP)
    pair_q = [net.send(GQ.at[:, :, sub(k)], RGQ.at[k - 1], me.in_group(k)) for k in subs]
    arrive(pair_q)

    def add_q(i, unused):
        p, t = i // G, lax.rem(i, G)
        total = GQ[p, t, s].astype(F32)
        for k in subs:
            total = total + RGQ[k - 1, p, t].astype(F32)
        RGQ[0, p, t] = total.astype(BF)
        return unused

    lax.fori_loop(0, nd * G, add_q, 0)
    z_q = [net.send(RGQ.at[0, plane(k)], ZGQ.at[k - 1], me.along_z(k)) for k in range(1, nd)]

    arrive(z_u)

    def total_u(t, unused):
        total = RGU[0, d, t].astype(F32)
        for k in range(1, nd):
            total = total + ZGU[k - 1, t].astype(F32)
        OGU[t] = total.astype(BF)
        return unused

    def stage_u(t, unused):
        total = RGU[0, d, t].astype(F32)
        for k in range(1, nd):
            total = total + ZGU[k - 1, t].astype(F32)
        ZGU[0, t] = total.astype(BF)
        return unused

    del total_u
    lax.fori_loop(0, G, stage_u, 0)
    OGU[g] = ZGU[0, g]
    plane_u = [net.send(ZGU.at[0, other(k)], OGU.at[g], me.in_plane(k)) for k in (1, 2, 3)]
    arrive(z_d)
    total = RGD[0, d].astype(F32)
    for k in range(1, nd):
        total = total + ZGD[k - 1].astype(F32)
    gd[...] = total
    arrive(z_o)
    total = OGO[d].astype(F32)
    for k in range(1, nd):
        total = total + ZGO[k - 1].astype(F32)
    go[...] = total

    keep = keep_column(keep_ref)
    arrive(outs)
    y = YO[...]
    for k in (1, 2, 3):
        y = y + RY[k - 1].astype(F32)
    layer_out[...] = (HS[...] + keep * y).astype(BF)
    arrive(sums)
    mine = pl.ds(pl.multiple_of(g * T, T), T)
    dxn1 = DXF[mine, :]
    for k in (1, 2, 3):
        dxn1 = dxn1 + RDX[k - 1].astype(F32)
    inputs = x_ref[...].astype(F32)
    scale1 = lax.rsqrt(jnp.mean(inputs * inputs, axis=-1, keepdims=True) + EPS)
    unit = inputs * scale1
    dxx = dxn1 * G12[0:1, :]
    tokens_grad[...] = (
        DH[...] + scale1 * (dxx - unit * jnp.mean(dxx * unit, axis=-1, keepdims=True))
    ).astype(BF)

    arrive(plane_u)
    for at, out in ((0, gg), (FG, gu)):
        out[...] = jnp.concatenate(
            [OGU[t, :, at + p * FB : at + (p + 1) * FB].astype(F32) for p in range(nd) for t in range(G)],
            axis=1,
        )
    arrive(z_q)

    def stage_q(t, unused):
        total = RGQ[0, d, t].astype(F32)
        for k in range(1, nd):
            total = total + ZGQ[k - 1, t].astype(F32)
        ZGQ[0, t] = total.astype(BF)
        return unused

    lax.fori_loop(0, G, stage_q, 0)
    OGQ[g] = ZGQ[0, g]
    plane_q = [net.send(ZGQ.at[0, other(k)], OGQ.at[g], me.in_plane(k)) for k in (1, 2, 3)]
    arrive(plane_q)
    parts = [OGQ[t].astype(F32) for t in range(G)]
    for at, out in ((0, gq), (QG, gk), (2 * QG, gv)):
        out[...] = jnp.concatenate([part[:, at : at + QG] for part in parts], axis=1)
    both = parts[0] + parts[1] + parts[2] + parts[3]
    ga[...] = column_to_row(both[:, QKV : QKV + 1])
    gm[...] = column_to_row(both[:, QKV + 1 : QKV + 2])
    net.finish()


class Sizes:
    pass


def tables(cf):
    lanes = np.arange(128) % (HD // 2)
    freq = THETA ** (-2.0 * lanes / HD)
    coarse = np.arange(cf.row_len // cf.T)[:, None] * cf.T * freq[None, :]
    fine = np.arange(cf.T)[:, None] * freq[None, :]
    stack = lambda a: np.stack([np.cos(a), np.sin(a)]).astype(np.float32)
    return stack(coarse), stack(fine)


def vmem(shape, dtype=BF):
    return jax.ShapeDtypeStruct(shape, dtype)


def call(kernel, cf, name, collective, outs, scratch, n_sems, args, smem=()):
    in_specs = [
        pl.BlockSpec(memory_space=pltpu.SMEM if i in smem else pltpu.VMEM) for i in range(len(args))
    ]
    return pl.pallas_call(
        functools.partial(kernel, cf),
        out_shape=[jax.ShapeDtypeStruct(shape, dtype) for shape, dtype in outs],
        in_specs=in_specs,
        out_specs=[pl.BlockSpec(memory_space=pltpu.VMEM) for unused in outs],
        scratch_shapes=[pltpu.VMEM(shape, dtype) for shape, dtype in scratch]
        + [pltpu.SemaphoreType.DMA((n_sems,)), pltpu.SemaphoreType.DMA((n_sems,))],
        compiler_params=pltpu.CompilerParams(collective_id=collective, has_side_effects=True),
        name=name,
    )(*args)


def body(
    nd, nb, tokens, attn_gain, q_weight, k_weight, v_weight, o_weight, mlp_gain, gate_weight, up_weight,
    down_weight, doc_lengths, keep, cotangent,
):
    cf = Sizes()
    cf.nd, cf.S = nd, nb // G
    cf.T, cf.D = tokens.shape
    cf.R, cf.RF = q_weight.shape[0], down_weight.shape[0]
    cf.FF = gate_weight.shape[1]
    cf.FG, cf.FB = cf.FF // G, cf.FF // (G * nd)
    cf.row_len = cf.T * nb
    cf.scale = 1.0 / math.sqrt(HD)
    T, D, S, R, RF, FG = cf.T, cf.D, cf.S, cf.R, cf.RF, cf.FG
    TT = G * T
    tab_m, tab_r = tables(cf)
    keep_row = keep.reshape(1, T)
    rows = (nd, G, S, R)
    many = 16 + 9 * nd + 12 * S

    WQ, W2, WOF, DYG, XG, XN1, QH, KV, LSE, MIX, HS, XN2, G12 = call(
        kernel_a, cf, "forward_attention", 0,
        [((D, QKVP), BF), (rows + (2 * FG,), BF), ((D, D), BF), ((G, T, D), BF), ((G, T, D), BF), ((G, T, D), BF),
         ((HG, TT, HD), BF), ((2 * HG, cf.row_len, HD), BF), ((HG, 8, TT), F32), ((T, D), BF), ((T, D), F32),
         ((T, D), BF), ((8, D), F32)],
        [(rows + (QKVP,), BF), (rows + (D,), BF), ((G, R, QKVP), BF), ((G, R, 2 * FG), BF), ((HD, cf.row_len), BF),
         ((HG, TT, HD), BF), ((G, T, QG), BF), ((G, T, QG), BF)],
        many,
        [tokens, cotangent, keep_row, doc_lengths, attn_gain.reshape(1, R), mlp_gain.reshape(1, R), q_weight,
         k_weight, v_weight, o_weight, gate_weight, up_weight, tab_m, tab_r],
        smem=(3,),
    )
    YS, YO, DH, DO, GU, GD, GO, MG = call(
        kernel_b, cf, "feed_forward", 1,
        [((G, T, D), BF), ((T, D), F32), ((T, D), F32), ((T, D), BF), ((D, 2 * FG), BF), ((FG, D), BF), ((D, D), BF),
         ((8, D), F32)],
        [((G, T, D), BF), ((nd, S, RF, D), BF), ((FG, D), BF), ((TT, FG), BF), ((TT, 2 * FG), BF), ((D, TT), BF),
         ((FG, TT), BF), ((D, T), BF), ((TT, D), F32), ((G, T, D), BF), ((3, T, D), BF)],
        many,
        [XN2, DYG, W2.reshape(D, 2 * FG), down_weight, HS, cotangent, keep_row, G12, WOF, MIX],
    )
    layer_out, tokens_grad, ga, gq, gk, gv, go, gm, gg, gu, gd = call(
        kernel_c, cf, "backward_attention", 2,
        [((T, D), BF), ((T, D), BF), ((1, R), F32), ((R, D), F32), ((R, D), F32), ((R, D), F32), ((R, D), F32),
         ((1, R), F32), ((R, cf.FF), F32), ((R, cf.FF), F32), ((RF, D), F32)],
        [((G, T, QG), BF), ((G, T, QG), BF), ((HG, TT, HD), BF), ((3, T, D), BF),
         ((S - 1, nd, G, R, 2 * FG), BF), ((S - 1, nd, RF, D), BF), ((S - 1, nd, G, R, D), BF),
         ((nd - 1, G, R, 2 * FG), BF), ((nd - 1, RF, D), BF), ((3, nd, R, D), BF), ((nd - 1, R, D), BF),
         ((G, R, 2 * FG), BF), ((nd, R, D), BF), ((HD, cf.row_len), BF), ((2 * HG, cf.row_len, HD), F32),
         ((HG, TT, HD), F32), ((S - 1, 2 * HG, TT, HD), BF), ((S - 1, 2 * HG, TT, HD), BF), ((TT, QKVP), BF),
         ((TT, D), F32), ((G, T, D), BF), ((3, T, D), BF), ((D, TT), BF), (rows + (QKVP,), BF),
         ((S - 1, nd, G, R, QKVP), BF), ((nd - 1, G, R, QKVP), BF), ((G, R, QKVP), BF)],
        many,
        [tokens, keep_row, doc_lengths, tab_m, tab_r, WQ, XG, XN1, QH, KV, LSE, HS, G12, YS, YO, DH, DO,
         GU.reshape(rows + (2 * FG,)), GD.reshape(nd, S, RF, D), GO.reshape(rows + (D,)), MG],
        smem=(2,),
    )
    return (
        layer_out, tokens_grad, ga.reshape(R), gq, gk, gv, go, gm.reshape(R), gg, gu, gd,
    )


def solution(mesh):
    both = ("dp", "blk")
    rows, flat = P(both, None), P(both)
    in_specs = (
        rows, flat, rows, rows, rows, rows, flat, rows, rows, rows, P("dp", None), flat, rows,
    )
    out_specs = (rows, rows, flat, rows, rows, rows, rows, flat, rows, rows, rows)
    step = functools.partial(body, mesh.shape["dp"], mesh.shape["blk"])
    return jax.shard_map(step, mesh=mesh, in_specs=in_specs, out_specs=out_specs, check_vma=False)
```
